32 devices in a mesh: flow: 16 (over z, y, x), group: 2 (over core).
Axes of the slice: x: 2, y: 2, z: 4, core: 2. Of those that a mesh axis runs over, the one named last changes fastest.
Arguments:
- density: float32 [64, 32, 256], P('flow', 'group'), may hold values from 0.8 to 1.2
- velocity: float32 [3, 64, 32, 256], P(None, 'flow', 'group'), may hold values from -0.5 to 0.5
- pressure: float32 [64, 32, 256], P('flow', 'group'), may hold values from 0.7 to 1.3
- wave_state: float32 [4, 8, 8, 8, 4096], P(None, None, None, None, ('flow', 'group')), may hold values from -1.8 to 1.8
- tables: float32 [4, 512, 512], replicated, may hold values from -0.75 to 0.75
- margin_element: int32 [32, 64], P(('flow', 'group')), may hold values from 0 to 4095, as said below
- margin_block: int32 [32, 64], P(('flow', 'group')), may hold values from 0 to 31
- margin_table: int32 [32, 64], P(('flow', 'group')), may hold values from 0 to 3
Outputs:
- flow_state: float32 [5, 64, 32, 256], P(None, 'flow', 'group')
- wave_out: float32 [4, 8, 8, 8, 4096], P(None, None, None, None, ('flow', 'group'))
- forcing: float32 [3, 8, 8, 8, 4096], P(None, None, None, None, ('flow', 'group'))
The draws below stay inside these ranges and needn't reach their ends.
Inputs may be any that keep to these rules, and one draw needn't show every extreme that they name: `margin_element`: global element ids; element e belongs to the device at position e // 128 along flow then group. In every device's row at most 4 entries name elements of one owner, and some owner receives exactly 4 entries from it.
All inputs are finite; a program needn't handle non-finite values.
Results may differ from the reference program's by a relative error of at most 0.0003.
Values sent between devices are 32-bit elements; how exact they have to be, the bound alone decides.
A program may use at most 128 MiB of HBM per device.

```python
import jax
import jax.numpy as jnp
import numpy as np
from jax import lax

NP = 8
CX = 4
CY = 16
NZ = 256
EY = 8
EZ = 16
CAP = 4
NW = 4
STEPS = 2
OV_DEV = 64
NX = 64
NY = 32
NBLK = 32
ELEMENTS = 4096
N_FLOW = 16
N_GROUP = 2


def draw_margin_element(key, part):
    devices = N_FLOW * N_GROUP
    slot_total = devices * CAP
    center_key, choose_key = jax.random.split(jax.random.fold_in(key, 11))
    center = jax.random.randint(center_key, (), 0, devices)
    hot_width = max(devices // 16, 2)

    def one_sender(sender_key, sender):
        sub_keys = jax.random.split(sender_key, 3)
        owner_index = jnp.arange(slot_total, dtype=jnp.int32) // CAP
        offset = (owner_index - center) % devices
        priority = jax.random.randint(sub_keys[0], (slot_total,), 0, 2)
        priority = jnp.where(offset < hot_width, 2, priority)
        priority = jnp.where(owner_index == (center + 3 * sender + hot_width) % devices, 3, priority)
        tiebreak = jax.random.permutation(sub_keys[1], slot_total)
        scores = priority * (slot_total + 1) + tiebreak
        chosen = jnp.sort(jax.lax.top_k(scores, OV_DEV)[1])
        element = chosen // CAP * (EY * EZ) + jax.random.randint(sub_keys[2], (OV_DEV,), 0, EY * EZ)
        return element.astype(jnp.int32)
    sender_keys = jax.random.split(choose_key, devices)
    return jax.vmap(one_sender)(sender_keys, jnp.arange(devices, dtype=jnp.int32))


def plant(drawn, stream_key, low, top_value):
    spot = [jax.random.randint(jax.random.fold_in(stream_key, axis), (), 0, length) for axis, length in enumerate(drawn.shape)]
    longest = drawn.shape.index(max(drawn.shape))
    beside = spot[:longest] + [(spot[longest] + 1) % drawn.shape[longest]] + spot[longest + 1:]
    return drawn.at[tuple(spot)].set(low).at[tuple(beside)].set(top_value)


def levels(key, shape, cuts, low, high):
    def one(position, shards_of):
        steps = jax.random.uniform(jax.random.fold_in(jax.random.fold_in(key, 6), position), (shards_of,), jnp.float32, low / len(cuts), high / len(cuts))
        return jnp.repeat(jnp.exp(steps), shape[position] // shards_of).reshape((-1,) + (1,) * (len(shape) - position - 1))

    factor_of = one(*cuts[0])
    for cut in cuts[1:]:
        factor_of = factor_of * one(*cut)
    return factor_of


def centred(rng, shape, spread, reach, cuts=(), kind=jnp.bfloat16):
    values = jax.random.normal(rng, shape, jnp.float32) * spread
    if len(cuts) > 0:
        values = levels(rng, shape, cuts, -0.22, 0.18) * values
    return jnp.clip(values, min=-reach, max=reach).astype(kind)


def setup_inputs(seed: int = 0) -> dict:
    streams_of = jax.random.split(jax.random.key(seed), 9)
    density = jnp.clip(0.8 + 0.40000004 * jax.random.uniform(streams_of[0], (NX, NY, NZ), jnp.float32) ** levels(streams_of[0], (NX, NY, NZ), ((0, 16), (1, 2)), -0.2, 0.2), 0.8, 1.2)
    velocity = jnp.clip(jax.random.uniform(streams_of[1], (3, NX, NY, NZ), jnp.float32, -0.5, 0.5) * levels(streams_of[1], (3, NX, NY, NZ), ((1, 16), (2, 2)), -0.4, 0.0), -0.5, 0.5)
    pressure = jnp.clip(0.7 + 0.59999996 * jax.random.uniform(streams_of[2], (NX, NY, NZ), jnp.float32) ** levels(streams_of[2], (NX, NY, NZ), ((0, 16), (1, 2)), -0.2, 0.2), 0.7, 1.3)
    wave_state = centred(streams_of[3], (4, NP, NP, NP, ELEMENTS), 0.3, 1.8, ((4, 32),), jnp.float32)
    tables = centred(streams_of[4], (NW, NP**3, NP**3), 0.125, 0.75, (), jnp.float32)
    margin_element = draw_margin_element(jax.random.fold_in(streams_of[8], 71), 0)
    margin_block = plant(jax.random.randint(streams_of[6], (N_FLOW * N_GROUP, OV_DEV), 0, NBLK), jax.random.fold_in(streams_of[6], 1), 0, NBLK - 1).astype(jnp.int32)
    margin_table = plant(jax.random.randint(streams_of[7], (N_FLOW * N_GROUP, OV_DEV), 0, NW), jax.random.fold_in(streams_of[7], 1), 0, NW - 1).astype(jnp.int32)
    return {"density": density, "velocity": velocity, "pressure": pressure, "wave_state": wave_state, "tables": tables, "margin_element": margin_element, "margin_block": margin_block, "margin_table": margin_table}


GAMMA = 1.4
DT_FLOW = 0.08
ACOUSTIC_STEP = 0.01
MAXIMUM_DEGREE = lax.Precision.HIGHEST

def legendre_pair(quadrature_nodes, degree):
    previous = np.ones(quadrature_nodes.shape[0])
    current = quadrature_nodes * 1.0
    for order in range(2, degree + 1):
        previous, current = (current, ((2 * order - 1) * quadrature_nodes * current - (order - 1) * previous) / order)
    return (previous, current)

def lobatto(point_count):
    degree = point_count - 1
    quadrature_nodes = -np.cos(np.pi * np.arange(point_count) / degree)
    for sweep in range(60):
        previous, current = legendre_pair(quadrature_nodes, degree)
        quadrature_nodes = quadrature_nodes - (quadrature_nodes * current - previous) / (point_count * current)
    previous, values = legendre_pair(quadrature_nodes, degree)
    quadrature_weights = 2.0 / (degree * (degree + 1) * values ** 2)
    identity = np.eye(point_count)
    differ = quadrature_nodes[:, None] - quadrature_nodes[None, :] + identity
    matrix = values[:, None] / values[None, :] / differ * (1.0 - identity)
    matrix[0, 0] = -degree * (degree + 1) / 4.0
    matrix[-1, -1] = degree * (degree + 1) / 4.0
    return (matrix, float(quadrature_weights[0]))

def physical(fields):
    density = fields[0]
    velocity = fields[1:4] / density
    pressure = (GAMMA - 1.0) * (fields[4] - 0.5 * density * lax.optimization_barrier(jnp.sum(velocity * velocity, axis=0)))
    return (density, velocity, pressure)

def euler_flux(fields, velocity, pressure, direction):
    normal = velocity[direction]
    components = [fields[0] * normal]
    for column in range(3):
        product = fields[1 + column] * normal
        if column == direction:
            product = product + pressure
        components.append(product)
    components.append((fields[4] + pressure) * normal)
    return jnp.stack(components)

def rusanov(left_side, right_side, direction):
    left_rho, left_vel, left_pre = physical(left_side)
    right_rho, right_vel, right_pre = physical(right_side)
    wave_speed = jnp.maximum(jnp.abs(left_vel[direction]) + jnp.sqrt(GAMMA * left_pre / left_rho), jnp.abs(right_vel[direction]) + jnp.sqrt(GAMMA * right_pre / right_rho))
    return 0.5 * (euler_flux(left_side, left_vel, left_pre, direction) + euler_flux(right_side, right_vel, right_pre, direction)) - 0.5 * wave_speed * (right_side - left_side)

def flow_rate(fields):
    tendency = jnp.zeros_like(fields)
    for direction in range(3):
        axis_index = direction + 1
        face_flux = rusanov(fields, jnp.roll(fields, -1, axis_index), direction)
        tendency = tendency - (face_flux - jnp.roll(face_flux, 1, axis_index))
    return tendency

def lamb_vector(fields):
    velocity = fields[1:4] / fields[0]
    slope_x = 0.5 * (jnp.roll(velocity, -1, 1) - jnp.roll(velocity, 1, 1))
    slope_y = 0.5 * (jnp.roll(velocity, -1, 2) - jnp.roll(velocity, 1, 2))
    slope_z = 0.5 * (jnp.roll(velocity, -1, 3) - jnp.roll(velocity, 1, 3))
    curl_x = slope_y[2] - slope_z[1]
    curl_y = slope_z[0] - slope_x[2]
    curl_z = slope_x[1] - slope_y[0]
    return jnp.stack([curl_y * velocity[2] - curl_z * velocity[1], curl_z * velocity[0] - curl_x * velocity[2], curl_x * velocity[1] - curl_y * velocity[0]])

def derivative(values, derive, direction):
    forms = ('ai,ijke->ajke', 'aj,ijke->iake', 'ak,ijke->ijae')
    return jnp.einsum(forms[direction], derive, values, precision=MAXIMUM_DEGREE)

def place_lifts(lower_lift, upper_lift, direction, point_count):
    middle_shape = list(upper_lift.shape)
    middle_shape.insert(direction, point_count - 2)
    middle = jnp.zeros(middle_shape, upper_lift.dtype)
    return jnp.concatenate([jnp.expand_dims(lower_lift, direction), middle, jnp.expand_dims(upper_lift, direction)], axis=direction)

def wave_rate(wave_field, forcing, upper_of, lower_of):
    point_count = wave_field.shape[1]
    matrix, end_weight = lobatto(point_count)
    derive = jnp.asarray(matrix, jnp.float32)
    pressure = wave_field[0]
    pressure_rate = jnp.zeros_like(pressure)
    velocity_tendency = []
    last = point_count - 1
    for direction in range(3):
        normal = wave_field[1 + direction]
        lower_face = jnp.stack([jnp.take(pressure, 0, axis=direction), jnp.take(normal, 0, axis=direction)])
        upper_face = jnp.stack([jnp.take(pressure, last, axis=direction), jnp.take(normal, last, axis=direction)])
        above_face = upper_of(lower_face, direction)
        below_face = lower_of(upper_face, direction)
        upper_pressure_flux = 0.5 * (upper_face[1] + above_face[1]) - 0.5 * (above_face[0] - upper_face[0])
        upper_normal_flux = 0.5 * (upper_face[0] + above_face[0]) - 0.5 * (above_face[1] - upper_face[1])
        lower_pressure_flux = 0.5 * (below_face[1] + lower_face[1]) - 0.5 * (lower_face[0] - below_face[0])
        lower_normal_flux = 0.5 * (below_face[0] + lower_face[0]) - 0.5 * (lower_face[1] - below_face[1])
        pressure_lift = place_lifts((lower_pressure_flux - lower_face[1]) / end_weight, -(upper_pressure_flux - upper_face[1]) / end_weight, direction, point_count)
        normal_lift = place_lifts((lower_normal_flux - lower_face[0]) / end_weight, -(upper_normal_flux - upper_face[0]) / end_weight, direction, point_count)
        pressure_rate = pressure_rate - derivative(normal, derive, direction) + pressure_lift
        velocity_tendency.append(-derivative(pressure, derive, direction) + normal_lift + forcing[direction])
    return jnp.stack([pressure_rate] + velocity_tendency)

def runge_kutta(start, rate, step_size):
    first_section = start + step_size * rate(start)
    second_section = 0.75 * start + 0.25 * (first_section + step_size * rate(first_section))
    return start / 3.0 + 2.0 / 3.0 * (second_section + step_size * rate(second_section))

def project(source, tables, margin_element, margin_block, margin_table):
    devices = N_FLOW * N_GROUP
    node_count = NP ** 3
    sorted_entries = source.reshape(3, N_FLOW, CX, N_GROUP, CY, NZ).transpose(0, 1, 3, 2, 4, 5)
    sorted_entries = sorted_entries.reshape(3, devices, NBLK, node_count)
    mapped_values = jnp.einsum('cdbn,tnm->tcdbm', sorted_entries, tables, precision=MAXIMUM_DEGREE)
    owners = jnp.broadcast_to(jnp.arange(devices, dtype=jnp.int32)[:, None], margin_block.shape)
    pieces = mapped_values[margin_table, :, owners, margin_block, :]
    summed = jax.ops.segment_sum(pieces.reshape(devices * OV_DEV, 3 * node_count), margin_element.reshape(-1), num_segments=ELEMENTS)
    return summed.reshape(ELEMENTS, 3, NP, NP, NP).transpose(1, 2, 3, 4, 0)

def shifted(faces, direction, offset):
    grid_view = faces.reshape(faces.shape[:3] + (N_FLOW * N_GROUP, EY, EZ))
    return jnp.roll(grid_view, offset, 3 + direction).reshape(faces.shape)

def reference(density, velocity, pressure, wave_state, tables, margin_element, margin_block, margin_table):
    momentum = density[None] * velocity
    energy = pressure / (GAMMA - 1.0) + 0.5 * density * lax.optimization_barrier(jnp.sum(velocity * velocity, axis=0))
    fields = jnp.concatenate([density[None], momentum, energy[None]], axis=0)
    wave_field = wave_state
    forcing = jnp.zeros((3, NP, NP, NP, ELEMENTS), jnp.float32)
    for step_index in range(STEPS):
        forcing = project(lamb_vector(fields), tables, margin_element, margin_block, margin_table)
        fields = runge_kutta(fields, flow_rate, DT_FLOW)
        wave_field = runge_kutta(wave_field, lambda current: wave_rate(current, forcing, lambda faces, direction: shifted(faces, direction, -1), lambda faces, direction: shifted(faces, direction, 1)), ACOUSTIC_STEP)
    return (fields, wave_field, forcing)
```

```python
import jax
import jax.numpy as jnp
import numpy as np
from jax import lax
from jax.experimental import pallas as pl
from jax.experimental.pallas import tpu as pltpu
from jax.sharding import PartitionSpec as P

NP = 8
EZ = 16
CAP = 4
STEPS = 2


GAMMA = 1.4
DT_FLOW = 0.08
ACOUSTIC_STEP = 0.01
MAXIMUM_DEGREE = lax.Precision.HIGHEST


def from_behind(value, axis, by):
    length = lax.axis_size(axis)
    return lax.ppermute(value, axis, [(i, (i + by) % length) for i in range(length)])


def legendre_pair(quadrature_nodes, degree):
    previous = np.ones(quadrature_nodes.shape[0])
    current = quadrature_nodes * 1.0
    for order in range(2, degree + 1):
        previous, current = (
            current,
            ((2 * order - 1) * quadrature_nodes * current - (order - 1) * previous) / order,
        )
    return (previous, current)


def lobatto(point_count):
    degree = point_count - 1
    quadrature_nodes = -np.cos(np.pi * np.arange(point_count) / degree)
    for sweep in range(60):
        previous, current = legendre_pair(quadrature_nodes, degree)
        quadrature_nodes = quadrature_nodes - (quadrature_nodes * current - previous) / (
            point_count * current
        )
    previous, values = legendre_pair(quadrature_nodes, degree)
    quadrature_weights = 2.0 / (degree * (degree + 1) * values**2)
    identity = np.eye(point_count)
    differ = quadrature_nodes[:, None] - quadrature_nodes[None, :] + identity
    matrix = values[:, None] / values[None, :] / differ * (1.0 - identity)
    matrix[0, 0] = -degree * (degree + 1) / 4.0
    matrix[-1, -1] = degree * (degree + 1) / 4.0
    return (matrix, float(quadrature_weights[0]))


XW = 3
YW = 4
VMEM = pltpu.VMEM


def wide_fields(fields):
    rows = fields.shape[2]
    below = from_behind(fields[:, :, rows - YW :], ("group",), 1)
    above = from_behind(fields[:, :, :YW], ("group",), -1)
    tall = jnp.concatenate([fields, above, below], axis=2)
    planes = fields.shape[1]
    before = from_behind(tall[:, planes - XW :], ("flow",), 1)
    after = from_behind(tall[:, :XW], ("flow",), -1)
    return jnp.concatenate([before, tall, after], axis=1)


def primitive(state):
    inverse = 1.0 / state[0]
    vel = [state[1 + d] * inverse for d in range(3)]
    square = vel[0] * vel[0] + vel[1] * vel[1] + vel[2] * vel[2]
    pressure = (GAMMA - 1.0) * (state[4] - 0.5 * state[0] * square)
    return vel, pressure, jnp.sqrt(GAMMA * pressure * inverse)


def flux_of(state, prim, d):
    vel, pressure, sound = prim
    normal = vel[d]
    parts = [state[d + 1]]
    parts[0] = state[0] * normal
    for c in range(3):
        product = state[1 + c] * normal
        parts.append(product + pressure if c == d else product)
    parts.append((state[4] + pressure) * normal)
    return parts, jnp.abs(normal) + sound


def face(left, right, left_flux, right_flux, left_speed, right_speed):
    speed = jnp.maximum(left_speed, right_speed)
    return [
        0.5 * (left_flux[c] + right_flux[c]) - 0.5 * speed * (right[c] - left[c])
        for c in range(5)
    ]


def flow_kernel(wide_ref, out_ref, first_ref, second_ref):
    def load(ref, plane):
        return [ref[c, plane] for c in range(5)]

    def stage(src, finish):
        count = src.shape[1] - 2

        def x_face(left, right):
            left_flux, left_speed = flux_of(left, primitive(left), 0)
            right_flux, right_speed = flux_of(right, primitive(right), 0)
            return face(left, right, left_flux, right_flux, left_speed, right_speed)

        def along(cell, prim, d, axis):
            size = cell[0].shape[axis]
            flux, speed = flux_of(cell, prim, d)
            back = lambda v: pltpu.roll(v, size - 1, axis)
            upper = face(
                cell,
                [back(v) for v in cell],
                flux,
                [back(v) for v in flux],
                speed,
                back(speed),
            )
            return [upper[c] - pltpu.roll(upper[c], 1, axis) for c in range(5)]

        def body(i, lower):
            cell = load(src, i + 1)
            upper = x_face(cell, load(src, i + 2))
            prim = primitive(cell)
            dy = along(cell, prim, 1, 0)
            dz = along(cell, prim, 2, 1)
            for c in range(5):
                rate = -(upper[c] - lower[c]) - dy[c] - dz[c]
                finish(i, c, cell[c] + DT_FLOW * rate)
            return upper

        lax.fori_loop(0, count, body, x_face(load(src, 0), load(src, 1)))

    def first(i, c, value):
        first_ref[c, i] = value

    def second(i, c, value):
        second_ref[c, i] = 0.75 * wide_ref[c, i + 2] + 0.25 * value

    def third(i, c, value):
        total = wide_ref[c, i + 3] * (1.0 / 3.0) + (2.0 / 3.0) * value
        out_ref[c, i] = total[: out_ref.shape[2]]

    stage(wide_ref, first)
    stage(first_ref, second)
    stage(second_ref, third)


def flow_step(wide, shape):
    planes, rows, columns = wide.shape[1:]
    return pl.pallas_call(
        flow_kernel,
        out_shape=jax.ShapeDtypeStruct(shape, jnp.float32),
        in_specs=[pl.BlockSpec(memory_space=VMEM)],
        out_specs=pl.BlockSpec(memory_space=VMEM),
        scratch_shapes=[
            pltpu.VMEM((5, planes - 2, rows, columns), jnp.float32),
            pltpu.VMEM((5, planes - 4, rows, columns), jnp.float32),
        ],
        cost_estimate=pl.CostEstimate(
            flops=40000000, bytes_accessed=4 * wide.size, transcendentals=0
        ),
        name="flow_step",
    )(wide)


def wave_kernel(matrix, lift, keep, gain, *refs):
    if keep:
        start_ref, cur, forcing, below_ref, above_ref, dcol, out = refs
    else:
        cur, forcing, below_ref, above_ref, dcol, out = refs
    n = cur.shape[1]
    last = n - 1
    lanes = cur.shape[-1]
    node = lax.broadcasted_iota(jnp.int32, (n, lanes), 0)
    z = lax.broadcasted_iota(jnp.int32, (n, lanes), 1) % EZ
    turn = lambda v, by: pltpu.roll(v, by % lanes, v.ndim - 1)

    def store(f, i, j, rate):
        value = gain * (cur[f, i, j] + ACOUSTIC_STEP * rate)
        if keep:
            value = keep * start_ref[f, i, j] + value
        out[f, i, j] = value

    for i in range(n):
        p7, u7 = cur[0, i, :, last, :], cur[3, i, :, last, :]
        p0, u0 = cur[0, i, :, 0, :], cur[3, i, :, 0, :]
        plus, minus = u7 + p7, u0 - p0
        below = jnp.where(z == 0, turn(plus, 1 - EZ), turn(plus, 1))
        above = jnp.where(z == EZ - 1, turn(minus, EZ - 1), turn(minus, -1))
        low_z = lift * (below - (u0 + p0))
        up_z = lift * (above - (u7 - p7))
        for j in range(n):
            p, u, v, w = (cur[f, i, j] for f in range(4))
            rate_p = jnp.zeros_like(p)
            rates = [forcing[d, i, j] for d in range(3)]
            for m in range(n):
                if matrix[i, m] != 0.0:
                    rate_p = rate_p - float(matrix[i, m]) * cur[1, m, j]
                    rates[0] = rates[0] - float(matrix[i, m]) * cur[0, m, j]
                if matrix[j, m] != 0.0:
                    rate_p = rate_p - float(matrix[j, m]) * cur[2, i, m]
                    rates[1] = rates[1] - float(matrix[j, m]) * cur[0, i, m]
                rate_p = rate_p - dcol[m] * cur[3, i, j, m : m + 1, :]
                rates[2] = rates[2] - dcol[m] * cur[0, i, j, m : m + 1, :]
            if i == 0:
                low = lift * (below_ref[j] - (u + p))
                rate_p, rates[0] = rate_p + low, rates[0] + low
            if i == last:
                up = lift * (above_ref[j] - (u - p))
                rate_p, rates[0] = rate_p - up, rates[0] + up
            if j == 0:
                low = lift * (turn(cur[2, i, last] + cur[0, i, last], EZ) - (v + p))
                rate_p, rates[1] = rate_p + low, rates[1] + low
            if j == last:
                up = lift * (turn(cur[2, i, 0] - cur[0, i, 0], -EZ) - (v - p))
                rate_p, rates[1] = rate_p - up, rates[1] + up
            low = jnp.where(node == 0, low_z[j : j + 1], 0.0)
            up = jnp.where(node == last, up_z[j : j + 1], 0.0)
            rate_p, rates[2] = rate_p + (low - up), rates[2] + (low + up)
            for f, rate in enumerate([rate_p] + rates):
                store(f, i, j, rate)


def wave_stage(start, current, forcing, keep, gain):
    n = current.shape[1]
    matrix, end_weight = lobatto(n)
    dcol = jnp.broadcast_to(
        jnp.asarray(matrix.T, jnp.float32)[:, :, None], (n, n, current.shape[-1])
    )
    axes = ("flow", "group")
    below = from_behind(current[1, n - 1] + current[0, n - 1], axes, 1)
    above = from_behind(current[1, 0] - current[0, 0], axes, -1)
    arguments = ([start] if keep else []) + [current, forcing, below, above, dcol]

    def body(*refs):
        wave_kernel(matrix, 0.5 / end_weight, keep, gain, *refs)

    return pl.pallas_call(
        body,
        out_shape=jax.ShapeDtypeStruct(current.shape, jnp.float32),
        in_specs=[pl.BlockSpec(memory_space=VMEM)] * len(arguments),
        out_specs=pl.BlockSpec(memory_space=VMEM),
        cost_estimate=pl.CostEstimate(
            flops=20000000, bytes_accessed=12 * current.size, transcendentals=0
        ),
        name="wave_stage",
    )(*arguments)


def wave_step(start, forcing):
    first = wave_stage(start, start, forcing, 0.0, 1.0)
    second = wave_stage(start, first, forcing, 0.75, 0.25)
    return wave_stage(start, second, forcing, 1.0 / 3.0, 2.0 / 3.0)


def routes(element_ids, block_ids, table_ids, block_count, table_count, local_count):
    devices = lax.axis_size("flow") * lax.axis_size("group")
    entry_count = element_ids.shape[0]
    owner_index = element_ids // local_count
    local_index = element_ids % local_count
    same_owner = owner_index[:, None] == owner_index[None, :]
    earlier = jnp.arange(entry_count)[:, None] > jnp.arange(entry_count)[None, :]
    slot_index = owner_index * CAP + jnp.sum(same_owner & earlier, axis=1)
    in_slot = jnp.arange(devices * CAP)[:, None] == slot_index[None, :]
    labels = jnp.sum(jnp.where(in_slot, local_index + 1, 0), axis=1) - 1
    column = table_ids * block_count + block_ids
    picked = jnp.sum(jnp.where(in_slot, column + 1, 0), axis=1) - 1
    pick = picked[:, None] == jnp.arange(table_count * block_count)[None, :]
    labels = lax.all_to_all(
        labels.reshape(devices, CAP), ("flow", "group"), split_axis=0, concat_axis=0, tiled=True
    )
    place = labels.reshape(-1)[:, None] == jnp.arange(local_count)[None, :]
    pick = pick.astype(jnp.float32).reshape(-1, table_count, block_count)
    return pick, place.astype(jnp.float32)


def gather_sources(source, tables, pick, place):
    node_count = tables.shape[1]
    blocks = source.reshape(3, -1, node_count)
    mapped = jnp.einsum("yki,xiq->xykq", blocks, tables, precision=MAXIMUM_DEGREE)
    rows = jnp.einsum("sxk,xykq->syq", pick, mapped, precision=MAXIMUM_DEGREE)
    devices = rows.shape[0] // CAP
    arrived = lax.all_to_all(
        rows.reshape(devices, CAP, 3, node_count),
        ("flow", "group"),
        split_axis=0,
        concat_axis=0,
        tiled=True,
    ).reshape(-1, 3, node_count)
    summed = jnp.einsum("ryq,re->yqe", arrived, place, precision=MAXIMUM_DEGREE)
    return summed.reshape(3, NP, NP, NP, place.shape[1])


def local(
    density, velocity, pressure, wave_state, tables, margin_element, margin_block, margin_table
):
    momentum = density[None] * velocity
    energy = pressure / (GAMMA - 1.0) + 0.5 * density * jnp.sum(velocity * velocity, axis=0)
    fields = jnp.concatenate([density[None], momentum, energy[None]], axis=0)
    wave_field = wave_state
    pick, place = routes(
        margin_element[0],
        margin_block[0],
        margin_table[0],
        density.size // tables.shape[1],
        tables.shape[0],
        wave_state.shape[-1],
    )
    rows = fields.shape[2]
    for step_index in range(STEPS):
        wide = wide_fields(fields)
        own = wide[:, XW:-XW]
        along_y = jnp.concatenate([own[:, :, -1:], own[:, :, : rows + 1]], axis=2)
        source = lamb_vector(fields, wide[:, XW - 1 : 1 - XW, :rows], along_y)
        forcing = gather_sources(source, tables, pick, place)
        fields = flow_step(wide, fields.shape)
        wave_field = wave_step(wave_field, forcing)
    return (fields, wave_field, forcing)


def lamb_vector(fields, along_x, along_y):
    velocity = fields[1:4] / fields[0]
    wide_x = along_x[1:4] / along_x[0]
    wide_y = along_y[1:4] / along_y[0]
    slope_x = 0.5 * (wide_x[:, 2:] - wide_x[:, :-2])
    slope_y = 0.5 * (wide_y[:, :, 2:] - wide_y[:, :, :-2])
    slope_z = 0.5 * (jnp.roll(velocity, -1, 3) - jnp.roll(velocity, 1, 3))
    curl_x = slope_y[2] - slope_z[1]
    curl_y = slope_z[0] - slope_x[2]
    curl_z = slope_x[1] - slope_y[0]
    return jnp.stack(
        [
            curl_y * velocity[2] - curl_z * velocity[1],
            curl_z * velocity[0] - curl_x * velocity[2],
            curl_x * velocity[1] - curl_y * velocity[0],
        ]
    )


def solution(mesh):
    in_specs = (
        P("flow", "group", None),
        P(None, "flow", "group", None),
        P("flow", "group", None),
        P(None, None, None, None, ("flow", "group")),
        P(),
        P(("flow", "group"), None),
        P(("flow", "group"), None),
        P(("flow", "group"), None),
    )
    out_specs = (
        P(None, "flow", "group", None),
        P(None, None, None, None, ("flow", "group")),
        P(None, None, None, None, ("flow", "group")),
    )
    return jax.shard_map(local, mesh=mesh, in_specs=in_specs, out_specs=out_specs, check_vma=False)
```
